32 devices in a mesh: mode: 8 (over z, x), var: 4 (over y, core).
Axes of the slice: x: 2, y: 2, z: 4, core: 2. Of those that a mesh axis runs over, the one named last changes fastest.
Arguments:
- control: bfloat16 [1, 4, 8, 1024, 1024], P(None, 'var', 'mode'), may hold values from -6 to 6
- filters: bfloat16 [3, 1024, 1024], replicated, may hold values from -4 to 5
- weights: bfloat16 [4, 3, 1024, 1024], P('var'), may hold values from 0.29882812 to 3
- vertical: bfloat16 [4, 64, 8], replicated, may hold values from -2 to 2
- balance: bfloat16 [3, 64, 64], replicated, may hold values from -0.75 to 0.75
Outputs:
- increment: bfloat16 [1, 4, 64, 1024, 1024], P(None, 'var', 'mode')
The draws below stay inside these ranges and needn't reach their ends.
All inputs are finite; a program needn't handle non-finite values.
Results may differ from the reference program's by a relative error of at most 0.006.
Values may be sent and summed in bfloat16 or wider, within the bound.
A program may use at most 128 MiB of HBM per device.

```python
import math
import jax
import jax.numpy as jnp
from jax import lax

MEMBERS = 1
NX = 1024
LEV = 64
FILTERS = 3
MODES = 8
VARS = 4


def draw_filters(key, part):
    index = jnp.arange(NX, dtype=jnp.float32)
    gap = index[:, None] - index[None, :]
    dense_scale = 0.25 / jnp.sqrt(jnp.float32(NX))
    mats = []
    for k, ratio in enumerate([128, 32, 8]):
        spread = NX / ratio
        envelope = jnp.exp(-(gap * gap) / (2.0 * spread * spread))
        scale_term = 1.0 / jnp.sqrt(spread * 1.7724539)
        sub = jax.random.fold_in(key, 11 + k)
        far_key = jax.random.fold_in(key, 31 + k)
        noise = jnp.clip(jax.random.normal(sub, (NX, NX), jnp.float32), -4.0, 4.0)
        dense = jnp.clip(jax.random.normal(far_key, (NX, NX), jnp.float32), -4.0, 4.0)
        mats.append(jnp.eye(NX, dtype=jnp.float32) + scale_term * envelope * noise + dense_scale * dense)
    return jnp.stack(mats).astype(jnp.bfloat16)


def block_levels(stream_key, shape, split, least, high):
    loudness = 1.0
    for axis_at, blocks in split:
        draws = jax.random.uniform(jax.random.fold_in(jax.random.fold_in(stream_key, 6), axis_at), (blocks,), jnp.float32, least / len(split), high / len(split))
        loudness = loudness * jnp.repeat(jnp.exp(draws), shape[axis_at] // blocks).reshape((-1,) + (1,) * (len(shape) - 1 - axis_at))
    return loudness


def centred(key, shape, scale, limit, split=(), kind=jnp.bfloat16):
    level = block_levels(key, shape, split, -0.22, 0.18) if split else 1.0
    drawn = jax.random.normal(key, shape, jnp.float32) * scale * level
    return jnp.minimum(jnp.maximum(drawn, -limit), limit).astype(kind)


def setup_inputs(seed: int = 0) -> dict:
    streams_of = jax.random.split(jax.random.key(seed), 6)
    return {
        "control": centred(streams_of[0], (MEMBERS, VARS, MODES, NX, NX), 1.0, 6.0, ((1, 4), (2, 8))),
        "filters": draw_filters(jax.random.fold_in(streams_of[5], 71), 0),
        "weights": jnp.clip(jnp.exp(math.log(3.0) - 2.306499 * jax.random.uniform(streams_of[2], (VARS, FILTERS, NX, NX), jnp.float32) ** block_levels(streams_of[2], (VARS, FILTERS, NX, NX), ((0, 4),), -0.2, 0.2)), 0.29882812, 3.0).astype(jnp.bfloat16),
        "vertical": centred(streams_of[3], (VARS, LEV, MODES), MODES ** -0.5, 2.0),
        "balance": centred(streams_of[4], (VARS - 1, LEV, LEV), LEV ** -0.5, 0.75),
    }


def smooth_plane(plane, filters, weights):
    total = jnp.zeros(plane.shape, jnp.float32)
    for k in range(FILTERS):
        half = jnp.dot(filters[k], plane, preferred_element_type=jnp.float32).astype(jnp.bfloat16)
        full = jnp.dot(half, filters[k].T, preferred_element_type=jnp.float32)
        total = total + weights[k].astype(jnp.float32) * full
    return total.astype(jnp.bfloat16)


def reference(control, filters, weights, vertical, balance):
    results = []
    for m in range(MEMBERS):
        filtered = []
        for v in range(VARS):
            planes = lax.map(lambda p: smooth_plane(p, filters, weights[v]), control[m, v])
            filtered.append(planes.reshape(MODES, NX * NX))
        stream_levels = jnp.dot(vertical[0], filtered[0], preferred_element_type=jnp.float32)
        stream = stream_levels.astype(jnp.bfloat16)
        outs = [stream]
        for v in range(1, VARS):
            levels = jnp.dot(vertical[v], filtered[v], preferred_element_type=jnp.float32)
            extra = jnp.dot(balance[v - 1], stream, preferred_element_type=jnp.float32)
            outs.append((levels + extra).astype(jnp.bfloat16))
        results.append(jnp.stack(outs).reshape(VARS, LEV, NX, NX))
    return jnp.stack(results)
```

```python
import jax
import jax.numpy as jnp
from jax import lax
from jax.sharding import PartitionSpec as P


def smooth(planes, filters, weights):
    total = jnp.zeros(planes.shape, jnp.float32)
    for k in range(filters.shape[0]):
        half = jnp.einsum(
            "ij,pjc->pic", filters[k], planes, preferred_element_type=jnp.float32
        ).astype(jnp.bfloat16)
        full = jnp.einsum("pic,dc->pid", half, filters[k], preferred_element_type=jnp.float32)
        total = total + weights[k].astype(jnp.float32) * full
    return total.astype(jnp.bfloat16)


def per_device_exchange(control, filters, weights, vertical, balance):
    members, _, depth, rows, cols = control.shape
    nmode = lax.axis_size("mode")
    nvar = lax.axis_size("var")
    strip = rows // (nmode * nvar)
    levcount = vertical.shape[1]
    filtered = smooth(control.reshape(members * depth, rows, cols), filters, weights[0])
    filtered = filtered.reshape(members, 1, depth, nvar, nmode, strip, cols)
    blocks = lax.all_to_all(
        lax.all_to_all(filtered, "mode", split_axis=4, concat_axis=2, tiled=True),
        "var",
        split_axis=3,
        concat_axis=1,
        tiled=True,
    )
    modecount = blocks.shape[2]
    blocks = blocks.reshape(members, nvar, modecount, strip * cols)
    levels = jnp.einsum("vlq,mvqc->mvlc", vertical, blocks, preferred_element_type=jnp.float32)
    stream = levels[:, 0].astype(jnp.bfloat16)
    extra = jnp.einsum("vlk,mkc->mvlc", balance, stream, preferred_element_type=jnp.float32)
    result = jnp.concatenate([levels[:, :1], levels[:, 1:] + extra], axis=1).astype(jnp.bfloat16)
    result = result.reshape(members, nvar, levcount, 1, 1, strip, cols)
    back = lax.all_to_all(
        lax.all_to_all(result, "mode", split_axis=2, concat_axis=4, tiled=True),
        "var",
        split_axis=1,
        concat_axis=3,
        tiled=True,
    )
    return back.reshape(members, 1, levcount // nmode, rows, cols)


def coefficients(vertical, balance, var, mode, nmode):
    nvar, levcount, _ = vertical.shape
    mine = levcount // nmode
    own = lax.dynamic_slice_in_dim(
        lax.dynamic_index_in_dim(vertical, var, 0, keepdims=False), mode * mine, mine, 0
    )
    regress = lax.dynamic_slice_in_dim(
        lax.dynamic_index_in_dim(balance, jnp.maximum(var - 1, 0), 0, keepdims=False),
        mode * mine, mine, 0,
    )
    folded = jnp.dot(
        regress.astype(jnp.float32), vertical[0].astype(jnp.float32), precision="highest"
    )
    folded = jnp.where(var > 0, folded, 0.0)
    high = folded.astype(jnp.bfloat16)
    low = (folded - high.astype(jnp.float32)).astype(jnp.bfloat16)
    return own, high, low


def per_device_gather(control, filters, weights, vertical, balance):
    members, _, depth, rows, cols = control.shape
    nmode = lax.axis_size("mode")
    var = lax.axis_index("var")
    filtered = smooth(control.reshape(members * depth, rows, cols), filters, weights[0])
    first = lax.psum(jnp.where(var == 0, filtered, jnp.zeros_like(filtered)), "var")
    both = jnp.stack([filtered, first]).reshape(2, members, depth, rows, cols)
    both = lax.all_gather(both, "mode", axis=2, tiled=True)
    own, high, low = coefficients(vertical, balance, var, lax.axis_index("mode"), nmode)
    coef = jnp.stack([own, high], axis=1)
    levels = jnp.einsum("lsq,smqrc->mlrc", coef, both, preferred_element_type=jnp.float32)
    levels += jnp.einsum("lq,mqrc->mlrc", low, both[1], preferred_element_type=jnp.float32)
    return levels.astype(jnp.bfloat16)[:, None]


def solution(mesh):
    in_specs = (P(None, "var", "mode", None, None), P(), P("var", None, None, None), P(), P())
    out_specs = P(None, "var", "mode", None, None)

    def run(control, filters, weights, vertical, balance):
        members, _, modes, rows, cols = control.shape
        gather = modes * mesh.shape["mode"] <= vertical.shape[1] * 2
        body = per_device_gather if gather else per_device_exchange
        return jax.shard_map(
            body, mesh=mesh, in_specs=in_specs, out_specs=out_specs, check_vma=False
        )(control, filters, weights, vertical, balance)

    return run
```

```python
import functools

import jax
import jax.numpy as jnp
from jax import lax
from jax.experimental import pallas as pl
from jax.experimental.pallas import tpu as pltpu
from jax.sharding import PartitionSpec as P


def smooth(planes, filters, weights):
    total = jnp.zeros(planes.shape, jnp.float32)
    for k in range(filters.shape[0]):
        half = jnp.einsum(
            "ij,pjc->pic", filters[k], planes, preferred_element_type=jnp.float32
        ).astype(jnp.bfloat16)
        full = jnp.einsum("pic,dc->pid", half, filters[k], preferred_element_type=jnp.float32)
        total = total + weights[k].astype(jnp.float32) * full
    return total.astype(jnp.bfloat16)


def per_device_exchange(control, filters, weights, vertical, balance):
    members, _, depth, rows, cols = control.shape
    nmode = lax.axis_size("mode")
    nvar = lax.axis_size("var")
    strip = rows // (nmode * nvar)
    levcount = vertical.shape[1]
    filtered = smooth(control.reshape(members * depth, rows, cols), filters, weights[0])
    filtered = filtered.reshape(members, 1, depth, nvar, nmode, strip, cols)
    blocks = lax.all_to_all(
        lax.all_to_all(filtered, "mode", split_axis=4, concat_axis=2, tiled=True),
        "var",
        split_axis=3,
        concat_axis=1,
        tiled=True,
    )
    modecount = blocks.shape[2]
    blocks = blocks.reshape(members, nvar, modecount, strip * cols)
    levels = jnp.einsum("vlq,mvqc->mvlc", vertical, blocks, preferred_element_type=jnp.float32)
    stream = levels[:, 0].astype(jnp.bfloat16)
    extra = jnp.einsum("vlk,mkc->mvlc", balance, stream, preferred_element_type=jnp.float32)
    result = jnp.concatenate([levels[:, :1], levels[:, 1:] + extra], axis=1).astype(jnp.bfloat16)
    result = result.reshape(members, nvar, levcount, 1, 1, strip, cols)
    back = lax.all_to_all(
        lax.all_to_all(result, "mode", split_axis=2, concat_axis=4, tiled=True),
        "var",
        split_axis=1,
        concat_axis=3,
        tiled=True,
    )
    return back.reshape(members, 1, levcount // nmode, rows, cols)


def coefficients(vertical, balance, var, mode, nmode):
    nvar, levcount, _ = vertical.shape
    mine = levcount // nmode
    own = lax.dynamic_slice_in_dim(
        lax.dynamic_index_in_dim(vertical, var, 0, keepdims=False), mode * mine, mine, 0
    )
    regress = lax.dynamic_slice_in_dim(
        lax.dynamic_index_in_dim(balance, jnp.maximum(var - 1, 0), 0, keepdims=False),
        mode * mine, mine, 0,
    )
    folded = jnp.dot(
        regress.astype(jnp.float32), vertical[0].astype(jnp.float32), precision="highest"
    )
    folded = jnp.where(var > 0, folded, 0.0)
    high = folded.astype(jnp.bfloat16)
    low = (folded - high.astype(jnp.float32)).astype(jnp.bfloat16)
    return own, high, low


GROUP = 16
LINE = 2


def gather_kernel(
    nmode, nvar, chunks, control, filters, weights, coef, out,
    buf, stage, recv, line_send, tree_send, out_sem,
):
    mode, var = lax.axis_index("mode"), lax.axis_index("var")
    z, x = mode // LINE, mode % LINE
    nz = nmode // LINE
    rows, cols = control.shape
    strip = rows // chunks
    own_lead = nz
    tree_lead = nz + 2

    even = var % 2 == 0
    peers = [
        (z < nz - 1, (mode + LINE, var)),
        (z > 0, (mode - LINE, var)),
        (var >= 0, (z * LINE + 1 - x, var)),
    ]
    first = var == 0
    tree = [(even, (mode, var + 1))] + [
        (first, (mode, jnp.int32(v))) for v in range(2, nvar, 2)
    ]

    barrier = pltpu.get_barrier_semaphore()
    count = jnp.int32(0)
    greet = peers + tree + [
        (jnp.logical_not(even), (mode, var - 1)),
        (jnp.logical_and(even, var > 0), (mode, jnp.int32(0))),
    ]
    for exists, device in greet:
        @pl.when(exists)
        def _(device=device):
            pl.semaphore_signal(
                barrier, inc=1, device_id=device, device_id_type=pl.DeviceIdType.MESH
            )
        count += exists.astype(jnp.int32)
    pl.semaphore_wait(barrier, count)

    def part(slot, j):
        return buf.at[slot, pl.ds(pl.multiple_of(j * strip, strip), strip)]

    def line_copy(way, slot, j):
        return pltpu.make_async_remote_copy(
            part(slot, j), part(slot, j), line_send.at[way, slot // LINE, j], recv.at[slot, j],
            device_id=peers[way][1], device_id_type=pl.DeviceIdType.MESH,
        )

    def tree_copy(way, q, j):
        source = jnp.where(first, q, q + nmode)
        return pltpu.make_async_remote_copy(
            part(source, j), part(q + nmode, j), tree_send.at[way, q, j], recv.at[q + nmode, j],
            device_id=tree[way][1], device_id_type=pl.DeviceIdType.MESH,
        )

    def await_part(slot, j):
        pltpu.make_async_copy(part(slot, j), part(slot, j), recv.at[slot, j]).wait()

    def send_line(ways, slot, j):
        for way in ways:
            @pl.when(peers[way][0])
            def _(way=way):
                line_copy(way, slot, j).start()

    def send_tree(q, j):
        for way in range(len(tree)):
            @pl.when(tree[way][0])
            def _(way=way):
                tree_copy(way, q, j).start()

    def compute(j):
        at = pl.ds(pl.multiple_of(j * strip, strip), strip)
        total = jnp.zeros((strip, cols), jnp.float32)
        for k in range(filters.shape[0]):
            half = jnp.dot(filters[k, at], control[...], preferred_element_type=jnp.float32)
            full = lax.dot_general(
                half.astype(jnp.bfloat16), filters[k], (((1,), (1,)), ((), ())),
                preferred_element_type=jnp.float32,
            )
            total += weights[k, at].astype(jnp.float32) * full
        buf[mode, at] = total.astype(jnp.bfloat16)

    levels = out.shape[0]

    def out_copy(j):
        at = pl.ds(pl.multiple_of(j * strip, strip), strip)
        return pltpu.make_async_copy(stage.at[j % 2], out.at[:, at], out_sem.at[j % 2])

    def combine(j):
        @pl.when(j >= 2)
        def _():
            out_copy(j - 2).wait()

        height = levels * GROUP

        def put(i, sums):
            stage[j % 2, :, pl.ds(pl.multiple_of(i * GROUP, GROUP), GROUP)] = sums.reshape(
                levels, GROUP, cols
            ).astype(jnp.bfloat16)

        def group(i):
            return pl.ds(pl.multiple_of(j * strip + i * GROUP, GROUP), GROUP)

        @pl.when(first)
        def _():
            @pl.loop(0, strip // GROUP)
            def _(i):
                planes = buf[:nmode, group(i)].reshape(nmode * GROUP, cols)
                put(i, jnp.dot(
                    coef[:height, : nmode * GROUP], planes, preferred_element_type=jnp.float32
                ))

        @pl.when(jnp.logical_not(first))
        def _():
            @pl.loop(0, strip // GROUP)
            def _(i):
                planes = buf[:, group(i)].reshape(2 * nmode * GROUP, cols)
                sums = jnp.dot(coef[...], planes, preferred_element_type=jnp.float32)
                put(i, sums[:height] + sums[height:])

        out_copy(j).start()

    def within(j):
        return jnp.logical_and(j >= 0, j < chunks)

    @pl.loop(0, chunks + tree_lead)
    def _(t):
        @pl.when(t < chunks)
        def _():
            compute(t)
            send_line((0, 1, 2), mode, t)

            @pl.when(first)
            def _():
                send_tree(mode, t)

        for d in range(1, nz):
            for way, step in ((0, -d), (1, d)):
                there = jnp.logical_and(z + step >= 0, z + step < nz)

                @pl.when(jnp.logical_and(there, within(t - d)))
                def _(way=way, step=step, d=d):
                    slot = mode + step * LINE
                    await_part(slot, t - d)
                    send_line((way, 2), slot, t - d)

                    @pl.when(first)
                    def _():
                        send_tree(slot, t - d)

        @pl.when(within(t - own_lead))
        def _():
            for line in range(nz):
                slot = line * LINE + 1 - x
                await_part(slot, t - own_lead)

                @pl.when(first)
                def _():
                    send_tree(slot, t - own_lead)

        @pl.when(within(t - tree_lead))
        def _():
            @pl.when(jnp.logical_not(first))
            def _():
                for q in range(nmode):
                    await_part(q + nmode, t - tree_lead)

                    @pl.when(even)
                    def _():
                        tree_copy(0, q, t - tree_lead).start()

            combine(t - tree_lead)

    for j in range(max(chunks - 2, 0), chunks):
        out_copy(j).wait()

    @pl.loop(0, chunks)
    def _(j):
        for line in range(nz):
            slot = line * LINE + x
            for way, sent in ((0, z >= line), (1, z <= line), (2, z >= 0)):
                @pl.when(jnp.logical_and(sent, peers[way][0]))
                def _(way=way):
                    line_copy(way, slot, j).wait_send()
        for q in range(nmode):
            for way in range(len(tree)):
                @pl.when(tree[way][0])
                def _(way=way):
                    tree_copy(way, q, j).wait_send()


def per_device_gather(control, filters, weights, vertical, balance):
    members, _, depth, rows, cols = control.shape
    nmode, nvar = lax.axis_size("mode"), lax.axis_size("var")
    var = lax.axis_index("var")
    own, high, low = coefficients(vertical, balance, var, lax.axis_index("mode"), nmode)
    levels = own.shape[0]
    coef = jnp.stack([jnp.stack([own, high], 1), jnp.stack([jnp.zeros_like(own), low], 1)])
    coef = coef[:, :, None, :, :, None] * jnp.eye(GROUP, dtype=coef.dtype)[:, None, None, :]
    coef = coef.reshape(2 * levels * GROUP, 2 * nmode * GROUP)
    chunks = max(rows // 128, 1)
    strip = rows // chunks
    vmem = pl.BlockSpec(memory_space=pltpu.VMEM)
    out = pl.pallas_call(
        functools.partial(gather_kernel, nmode, nvar, chunks),
        out_shape=jax.ShapeDtypeStruct((levels, rows, cols), jnp.bfloat16),
        in_specs=[vmem] * 4,
        out_specs=pl.BlockSpec(memory_space=pl.ANY),
        scratch_shapes=[
            pltpu.VMEM((2 * nmode, rows, cols), jnp.bfloat16),
            pltpu.VMEM((2, levels, strip, cols), jnp.bfloat16),
            pltpu.SemaphoreType.DMA((2 * nmode, chunks)),
            pltpu.SemaphoreType.DMA((3, nmode // LINE, chunks)),
            pltpu.SemaphoreType.DMA((max(nvar // 2, 1), nmode, chunks)),
            pltpu.SemaphoreType.DMA((2,)),
        ],
        compiler_params=pltpu.CompilerParams(
            collective_id=0, has_side_effects=True, vmem_limit_bytes=64 * 1000 * 1000
        ),
    )(control.reshape(rows, cols), filters, weights[0], coef)
    return out.reshape(members, 1, levels, rows, cols)


def solution(mesh):
    in_specs = (P(None, "var", "mode", None, None), P(), P("var", None, None, None), P(), P())
    out_specs = P(None, "var", "mode", None, None)
    nmode, nvar = mesh.shape["mode"], mesh.shape["var"]

    def run(control, filters, weights, vertical, balance):
        members, _, modes, rows, cols = control.shape
        planes = 2 * modes + 2 * filters.shape[0] + 1 + 2 * vertical.shape[1] // nmode // 8
        gather = members == 1 and modes == nmode and nmode % LINE == 0 and nvar % 2 == 0
        gather = gather and planes * rows * cols * 2 <= 56 * 2**20
        body = per_device_gather if gather else per_device_exchange
        return jax.shard_map(
            body, mesh=mesh, in_specs=in_specs, out_specs=out_specs, check_vma=False
        )(control, filters, weights, vertical, balance)

    return run
```

```python
import functools

import jax
import jax.numpy as jnp
from jax import lax
from jax.experimental import pallas as pl
from jax.experimental.pallas import tpu as pltpu
from jax.sharding import PartitionSpec as P


def smooth(planes, filters, weights):
    total = jnp.zeros(planes.shape, jnp.float32)
    for k in range(filters.shape[0]):
        half = jnp.einsum(
            "ij,pjc->pic", filters[k], planes, preferred_element_type=jnp.float32
        ).astype(jnp.bfloat16)
        full = jnp.einsum("pic,dc->pid", half, filters[k], preferred_element_type=jnp.float32)
        total = total + weights[k].astype(jnp.float32) * full
    return total.astype(jnp.bfloat16)


def per_device_exchange(control, filters, weights, vertical, balance):
    members, _, depth, rows, cols = control.shape
    nmode = lax.axis_size("mode")
    nvar = lax.axis_size("var")
    strip = rows // (nmode * nvar)
    levcount = vertical.shape[1]
    filtered = smooth(control.reshape(members * depth, rows, cols), filters, weights[0])
    filtered = filtered.reshape(members, 1, depth, nvar, nmode, strip, cols)
    blocks = lax.all_to_all(
        lax.all_to_all(filtered, "mode", split_axis=4, concat_axis=2, tiled=True),
        "var",
        split_axis=3,
        concat_axis=1,
        tiled=True,
    )
    modecount = blocks.shape[2]
    blocks = blocks.reshape(members, nvar, modecount, strip * cols)
    levels = jnp.einsum("vlq,mvqc->mvlc", vertical, blocks, preferred_element_type=jnp.float32)
    stream = levels[:, 0].astype(jnp.bfloat16)
    extra = jnp.einsum("vlk,mkc->mvlc", balance, stream, preferred_element_type=jnp.float32)
    result = jnp.concatenate([levels[:, :1], levels[:, 1:] + extra], axis=1).astype(jnp.bfloat16)
    result = result.reshape(members, nvar, levcount, 1, 1, strip, cols)
    back = lax.all_to_all(
        lax.all_to_all(result, "mode", split_axis=2, concat_axis=4, tiled=True),
        "var",
        split_axis=1,
        concat_axis=3,
        tiled=True,
    )
    return back.reshape(members, 1, levcount // nmode, rows, cols)


def coefficients(vertical, balance, var, mode, nmode):
    nvar, levcount, _ = vertical.shape
    mine = levcount // nmode
    own = lax.dynamic_slice_in_dim(
        lax.dynamic_index_in_dim(vertical, var, 0, keepdims=False), mode * mine, mine, 0
    )
    regress = lax.dynamic_slice_in_dim(
        lax.dynamic_index_in_dim(balance, jnp.maximum(var - 1, 0), 0, keepdims=False),
        mode * mine, mine, 0,
    )
    folded = jnp.dot(
        regress.astype(jnp.float32), vertical[0].astype(jnp.float32), precision="highest"
    )
    folded = jnp.where(var > 0, folded, 0.0)
    high = folded.astype(jnp.bfloat16)
    low = (folded - high.astype(jnp.float32)).astype(jnp.bfloat16)
    return own, high, low


GROUP = 16
LINE = 2


def gather_kernel(
    nmode, nvar, chunks, control_in, filters_in, weights_in, coef, out,
    buf, stage, control, filters, weights,
    recv, line_send, tree_send, cross_send, out_sem, in_sem,
):
    mode, var = lax.axis_index("mode"), lax.axis_index("var")
    z, x = mode // LINE, mode % LINE
    nz = nmode // LINE
    rows, cols = control.shape
    strip = rows // chunks
    short = chunks - chunks // 8
    lead = 0
    line_lag = lead + nz + 2
    own_tree_lag = line_lag + 1
    tree_lag = line_lag + 2

    loads = [pltpu.make_async_copy(control_in, control, in_sem.at[0])]
    loads += [
        pltpu.make_async_copy(filters_in.at[k], filters.at[k], in_sem.at[2 * k + 1])
        for k in range(filters.shape[0])
    ]
    fetches = [
        pltpu.make_async_copy(weights_in.at[k], weights.at[k], in_sem.at[2 * k + 2])
        for k in range(filters.shape[0])
    ]
    for load in loads + fetches:
        load.start()

    first = var == 0
    even = var % 2 == 0
    later = jnp.logical_and(even, var > 0)
    peers = [
        (z < nz - 1, (mode + LINE, var)),
        (z > 0, (mode - LINE, var)),
        (var >= 0, (z * LINE + 1 - x, var)),
    ]
    tree = [(even, (mode, var + 1))] + [
        (first, (mode, jnp.int32(v))) for v in range(2, nvar, 2)
    ]

    barrier = pltpu.get_barrier_semaphore()
    count = jnp.int32(0)
    greet = peers + tree + [
        (jnp.logical_not(even), (mode, var - 1)),
        (later, (mode, jnp.int32(0))),
    ]
    for exists, device in greet:
        @pl.when(exists)
        def _(device=device):
            pl.semaphore_signal(
                barrier, inc=1, device_id=device, device_id_type=pl.DeviceIdType.MESH
            )
        count += exists.astype(jnp.int32)
    pl.semaphore_wait(barrier, count)

    def part(slot, j):
        return buf.at[slot, pl.ds(pl.multiple_of(j * strip, strip), strip)]

    def remote(source, slot, j, send_sem, device):
        return pltpu.make_async_remote_copy(
            part(source, j), part(slot, j), send_sem, recv.at[slot, j],
            device_id=device, device_id_type=pl.DeviceIdType.MESH,
        )

    def line_copy(way, slot, j):
        return remote(slot, slot, j, line_send.at[way, slot, j], peers[way][1])

    def tree_copy(way, q, j):
        source = jnp.where(first, q, q + nmode)
        return remote(source, q + nmode, j, tree_send.at[way, q, j], tree[way][1])

    def cross_copy(line, j):
        q = line * LINE + x
        return remote(q + nmode, q + nmode, j, cross_send.at[line, j], peers[2][1])

    def await_part(slot, j):
        pltpu.make_async_copy(part(slot, j), part(slot, j), recv.at[slot, j]).wait()

    def send_line(ways, slot, j):
        for way in ways:
            @pl.when(peers[way][0])
            def _(way=way):
                line_copy(way, slot, j).start()

    def send_tree(own_line, q, j):
        @pl.when(first)
        def _():
            tree_copy(0, q, j).start()
            if own_line:
                for way in range(1, len(tree)):
                    tree_copy(way, q, j).start()
            else:
                @pl.when(j < short)
                def _():
                    for way in range(1, len(tree)):
                        tree_copy(way, q, j).start()

    depth = min(2 * strip, rows)

    def compute(i):
        at = pl.ds(pl.multiple_of(i * depth, depth), depth)
        total = jnp.zeros((depth, cols), jnp.float32)
        for k in range(filters.shape[0]):
            @pl.when(i == 0)
            def _(k=k):
                if k == 0:
                    loads[0].wait()
                loads[k + 1].wait()

            half = jnp.dot(filters[k, at], control[...], preferred_element_type=jnp.float32)
            full = lax.dot_general(
                half.astype(jnp.bfloat16), filters[k], (((1,), (1,)), ((), ())),
                preferred_element_type=jnp.float32,
            )

            @pl.when(i == 0)
            def _(k=k):
                fetches[k].wait()

            total += weights[k, at].astype(jnp.float32) * full
        buf[mode, at] = total.astype(jnp.bfloat16)

    levels = out.shape[0]

    def out_copy(j):
        at = pl.ds(pl.multiple_of(j * strip, strip), strip)
        return pltpu.make_async_copy(stage.at[j % 2], out.at[:, at], out_sem.at[j % 2])

    def combine(j):
        @pl.when(j >= 2)
        def _():
            out_copy(j - 2).wait()

        height = levels * GROUP

        def put(i, sums):
            stage[j % 2, :, pl.ds(pl.multiple_of(i * GROUP, GROUP), GROUP)] = sums.reshape(
                levels, GROUP, cols
            ).astype(jnp.bfloat16)

        def group(i):
            return pl.ds(pl.multiple_of(j * strip + i * GROUP, GROUP), GROUP)

        @pl.when(first)
        def _():
            @pl.loop(0, strip // GROUP)
            def _(i):
                planes = buf[:nmode, group(i)].reshape(nmode * GROUP, cols)
                put(i, jnp.dot(
                    coef[:height, : nmode * GROUP], planes, preferred_element_type=jnp.float32
                ))

        @pl.when(jnp.logical_not(first))
        def _():
            @pl.loop(0, strip // GROUP)
            def _(i):
                planes = buf[:, group(i)].reshape(2 * nmode * GROUP, cols)
                sums = jnp.dot(coef[...], planes, preferred_element_type=jnp.float32)
                put(i, sums[:height] + sums[height:])

        out_copy(j).start()

    def within(j):
        return jnp.logical_and(j >= 0, j < chunks)

    def arrivals(t):
        for d in range(1, nz):
            j = t - lead - d
            for way, step in ((0, -d), (1, d)):
                there = jnp.logical_and(z + step >= 0, z + step < nz)
                there = jnp.logical_and(there, within(j))

                @pl.when(there)
                def _(way=way, step=step, j=j):
                    slot = mode + step * LINE
                    await_part(slot, j)
                    send_line((way, 2), slot, j)
                    send_tree(True, slot, j)

    @pl.loop(0, chunks + tree_lag)
    def _(t):
        @pl.when(t < chunks)
        def _():
            @pl.when(t % (depth // strip) == 0)
            def _():
                compute(t // (depth // strip))

            send_line((2, 0, 1), mode, t)
            send_tree(True, mode, t)

        arrivals(t)

        @pl.when(within(t - line_lag))
        def _():
            for line in range(nz):
                slot = line * LINE + 1 - x
                await_part(slot, t - line_lag)
                send_tree(False, slot, t - line_lag)

        @pl.when(jnp.logical_and(later, within(t - own_tree_lag)))
        def _():
            j = t - own_tree_lag
            for line in range(nz):
                q = line * LINE + x
                await_part(q + nmode, j)

                @pl.when(j >= short)
                def _():
                    cross_copy(line, j).start()

                tree_copy(0, q, j).start()

        @pl.when(within(t - tree_lag))
        def _():
            j = t - tree_lag

            @pl.when(later)
            def _():
                for line in range(nz):
                    q = line * LINE + 1 - x
                    await_part(q + nmode, j)
                    tree_copy(0, q, j).start()

            @pl.when(jnp.logical_not(even))
            def _():
                for q in range(nmode):
                    await_part(q + nmode, j)

            combine(j)

    for j in range(max(chunks - 2, 0), chunks):
        out_copy(j).wait()

    @pl.loop(0, chunks)
    def _(j):
        for line in range(nz):
            mine, other = line * LINE + x, line * LINE + 1 - x
            for way, sent in ((0, z >= line), (1, z <= line)):
                @pl.when(jnp.logical_and(sent, peers[way][0]))
                def _(way=way):
                    line_copy(way, mine, j).wait_send()

            line_copy(2, mine, j).wait_send()

            @pl.when(jnp.logical_and(later, j >= short))
            def _():
                cross_copy(line, j).wait_send()

            @pl.when(even)
            def _():
                tree_copy(0, mine, j).wait_send()
                tree_copy(0, other, j).wait_send()

            @pl.when(first)
            def _():
                for way in range(1, len(tree)):
                    tree_copy(way, mine, j).wait_send()

                @pl.when(j < short)
                def _():
                    for way in range(1, len(tree)):
                        tree_copy(way, other, j).wait_send()


def per_device_gather(control, filters, weights, vertical, balance):
    members, _, depth, rows, cols = control.shape
    nmode, nvar = lax.axis_size("mode"), lax.axis_size("var")
    var = lax.axis_index("var")
    own, high, low = coefficients(vertical, balance, var, lax.axis_index("mode"), nmode)
    levels = own.shape[0]
    coef = jnp.stack([jnp.stack([own, high], 1), jnp.stack([jnp.zeros_like(own), low], 1)])
    coef = coef[:, :, None, :, :, None] * jnp.eye(GROUP, dtype=coef.dtype)[:, None, None, :]
    coef = coef.reshape(2 * levels * GROUP, 2 * nmode * GROUP)
    chunks = max(rows // 64, 1)
    strip = rows // chunks
    vmem = pl.BlockSpec(memory_space=pltpu.VMEM)
    out = pl.pallas_call(
        functools.partial(gather_kernel, nmode, nvar, chunks),
        out_shape=jax.ShapeDtypeStruct((levels, rows, cols), jnp.bfloat16),
        in_specs=[pl.BlockSpec(memory_space=pl.ANY)] * 3 + [vmem],
        out_specs=pl.BlockSpec(memory_space=pl.ANY),
        scratch_shapes=[
            pltpu.VMEM((2 * nmode, rows, cols), jnp.bfloat16),
            pltpu.VMEM((2, levels, strip, cols), jnp.bfloat16),
            pltpu.VMEM((rows, cols), jnp.bfloat16),
            pltpu.VMEM(filters.shape, jnp.bfloat16),
            pltpu.VMEM(filters.shape, jnp.bfloat16),
            pltpu.SemaphoreType.DMA((2 * nmode, chunks)),
            pltpu.SemaphoreType.DMA((3, nmode, chunks)),
            pltpu.SemaphoreType.DMA((nvar // 2, nmode, chunks)),
            pltpu.SemaphoreType.DMA((nmode // LINE, chunks)),
            pltpu.SemaphoreType.DMA((2,)),
            pltpu.SemaphoreType.DMA((2 * filters.shape[0] + 1,)),
        ],
        compiler_params=pltpu.CompilerParams(
            collective_id=0, has_side_effects=True, vmem_limit_bytes=64 * 1000 * 1000
        ),
    )(control.reshape(rows, cols), filters, weights[0], coef)
    return out.reshape(members, 1, levels, rows, cols)


def solution(mesh):
    in_specs = (P(None, "var", "mode", None, None), P(), P("var", None, None, None), P(), P())
    out_specs = P(None, "var", "mode", None, None)
    nmode, nvar = mesh.shape["mode"], mesh.shape["var"]

    def run(control, filters, weights, vertical, balance):
        members, _, modes, rows, cols = control.shape
        planes = 2 * modes + 2 * filters.shape[0] + 1 + 2 * vertical.shape[1] // nmode // 8
        gather = members == 1 and modes == nmode and nmode % LINE == 0 and nvar % 2 == 0
        gather = gather and planes * rows * cols * 2 <= 56 * 2**20
        body = per_device_gather if gather else per_device_exchange
        return jax.shard_map(
            body, mesh=mesh, in_specs=in_specs, out_specs=out_specs, check_vma=False
        )(control, filters, weights, vertical, balance)

    return run
```
